128 devices in a mesh: item: 16 (over y, z_lo, core), tbl: 8 (over z_hi, x).
Axes of the slice: x: 4, y: 4, z: 4 (z_hi: 2, z_lo: 2; z = z_hi * 2 + z_lo), core: 2. Of those that a mesh axis runs over, the one named last changes fastest.
Arguments:
- tables: bfloat16 [16, 8192, 128], P('tbl'), may hold values from -2.5 to 2.5
- feat_ids: int32 [131072, 16, 8], P('item', 'tbl'), may hold values from 0 to 8191
- bag_lens: int32 [131072, 16], P('item', 'tbl'), may hold values from 1 to 8
- w_hidden: bfloat16 [2048, 1024], replicated, may hold values from -0.125 to 0.125
- b_hidden: float32 [1024], replicated, may hold values from -3 to 3
- w_out: bfloat16 [1024, 256], replicated, may hold values from -0.1875 to 0.1875
- b_out: float32 [256], replicated, may hold values from -3 to 3
- item_vecs: bfloat16 [4096, 256], P('item'), may hold values from -30 to 30
- elig_mask: int32 [256, 32], P(('item', 'tbl')), may hold values from 0 to 1, as said below
- positives: int32 [131072], P(('item', 'tbl')), may hold values from 0 to 4095, as said below
Outputs:
- user_loss: float32 [131072], P(('item', 'tbl'))
- user_grad: float32 [131072, 256], P(('item', 'tbl'))
- item_grad: float32 [4096, 256], P(('item', 'tbl'))
The draws below stay inside these ranges and needn't reach their ends.
Inputs may be any that keep to these rules, and one draw needn't show every extreme that they name: Every row of elig_mask holds at least one 1. elig_mask[u // 512, positives[u] // 128] = 1 for every user u.
All inputs are finite; a program needn't handle non-finite values.
Results may differ from the reference program's by a relative error of at most 0.03.
Values may be sent and summed in bfloat16 or wider, within the bound.
No kernel may reach another device: no remote copies, remote signals or barrier semaphores. Data moves between devices by JAX's collectives and lax.ppermute only.
A program may use at most 64 MiB of HBM per device.

```python
import math
import jax
import jax.numpy as jnp
import numpy as np
from jax import lax

E = 128
ROWS = 8192
BAG = 8
HID = 1024
DQ = 256
UBLK = 512
IBLK = 128
FEATS = 16
USERS = 131072
ITEMS = 4096


def eligibility(key):
    block_count = USERS // UBLK
    column_count = ITEMS // IBLK
    key_list = jax.random.split(jax.random.fold_in(key, 11), 5)
    density = jax.random.randint(key_list[0], (block_count, 1), 10, 101)
    rolled = jax.random.randint(key_list[1], (block_count, column_count), 0, 100)
    forced = jax.random.randint(key_list[2], (block_count, 1), 0, column_count)
    columns = jnp.arange(column_count, dtype=jnp.int32)[None, :]
    eligible = jnp.logical_or(rolled < density, columns == forced).astype(jnp.int32)
    counts = jnp.sum(eligible, axis=1)
    rank_table = jnp.cumsum(eligible, axis=1) - 1
    owner_block = jnp.arange(USERS, dtype=jnp.int32) // UBLK
    pick_rank = jax.random.randint(key_list[3], (USERS,), 0, 1048576) % counts[owner_block]
    user_rows = eligible[owner_block]
    user_ranks = rank_table[owner_block]
    chosen = jnp.sum(jnp.where(jnp.logical_and(user_rows > 0, user_ranks == pick_rank[:, None]), columns, 0), axis=1)
    within = jax.random.randint(key_list[4], (USERS,), 0, IBLK)
    return (eligible, (chosen * IBLK + within).astype(jnp.int32))


def draw_elig_mask(key, part):
    return eligibility(key)[0]


def draw_positives(key, part):
    return eligibility(key)[1]


def draw_item_vecs(key, part):
    key_list = jax.random.split(jax.random.fold_in(key, 23), 1)
    return (jax.random.normal(key_list[0], (ITEMS, DQ), jnp.float32) * 0.1).astype(jnp.bfloat16)


def place_ends(entries, own_key, low, high):
    longest = entries.shape.index(max(entries.shape))
    spots = []
    for shift in (0, 1):
        where = [jax.random.randint(jax.random.fold_in(own_key, axis), (), 0, length) for axis, length in enumerate(entries.shape)]
        where[longest] = (where[longest] + shift) % entries.shape[longest]
        spots.append(tuple(where))
    return entries.at[spots[0]].set(low).at[spots[1]].set(high)


def level_of(own_key, shape, cuts, least, top_value):
    level = 1.0
    for position, blocks in cuts:
        steps = jax.random.uniform(jax.random.fold_in(jax.random.fold_in(own_key, 6), position), (blocks,), jnp.float32, least / len(cuts), top_value / len(cuts))
        level = level * jnp.repeat(jnp.exp(steps), shape[position] // blocks).reshape((-1,) + (1,) * (len(shape) - 1 - position))
    return level


def cumulative_ranks(number_of, lean):
    portions = [(1 << 20) // math.isqrt(rank ** lean) + 1 for rank in range(1, number_of + 1)]
    scale = 1 + sum(portions) // (1 << 30)
    return np.cumsum(np.array([max(1, weight // scale) for weight in portions]))


def ranked(key, extent, amount, skew):
    table = cumulative_ranks(amount, skew)
    pick = jax.random.randint(jax.random.fold_in(key, 1), extent, 0, int(table[amount - 1]))
    grade = jnp.searchsorted(jnp.asarray(table, jnp.int32), pick, side="right")
    return jax.random.permutation(jax.random.fold_in(key, 2), amount)[grade].astype(jnp.int32)


def gaussian(rng, shape, spread, most, cuts=(), kind=jnp.bfloat16):
    drawn = jax.random.normal(rng, shape, jnp.float32) * spread
    if len(cuts) > 0:
        drawn = level_of(rng, shape, cuts, -0.22, 0.18) * drawn
    return jnp.clip(drawn, min=-most, max=most).astype(kind)


def setup_inputs(seed: int = 0) -> dict:
    key_of = jax.random.split(jax.random.key(seed), 11)
    return {
        "tables": gaussian(key_of[0], (FEATS, ROWS, E), 0.35, 2.5, ((0, 8),)),
        "feat_ids": place_ends(ranked(key_of[1], (USERS, FEATS, BAG), ROWS, 2), jax.random.fold_in(key_of[1], 3), 0, ROWS - 1).astype(jnp.int32),
        "bag_lens": place_ends(jax.random.randint(key_of[2], (USERS, FEATS), 1, BAG + 1), jax.random.fold_in(key_of[2], 1), 1, BAG).astype(jnp.int32),
        "w_hidden": gaussian(key_of[3], (FEATS * E, HID), (FEATS * E) ** -0.5, 0.125),
        "b_hidden": gaussian(key_of[4], (HID,), 0.5, 3.0, (), jnp.float32),
        "w_out": gaussian(key_of[5], (HID, DQ), HID ** -0.5, 0.1875),
        "b_out": gaussian(key_of[6], (DQ,), 0.3, 3.0, (), jnp.float32),
        "item_vecs": draw_item_vecs(jax.random.fold_in(key_of[10], 71), 0),
        "elig_mask": draw_elig_mask(jax.random.fold_in(key_of[10], 71), 0),
        "positives": draw_positives(jax.random.fold_in(key_of[10], 71), 0),
    }


masked_value = -1.0e30


def pool_feature(table, bag_ids, bag_count):
    gathered = jnp.take(table, bag_ids, axis=0).astype(jnp.float32)
    in_bag = jnp.arange(BAG, dtype=jnp.int32)[None, :] < bag_count[:, None]
    return jnp.sum(jnp.where(in_bag[:, :, None], gathered, 0.0), axis=1).astype(jnp.bfloat16)


def reference(tables, feat_ids, bag_lens, w_hidden, b_hidden, w_out, b_out, item_vecs, elig_mask, positives):
    pooled = lax.map(lambda feature: pool_feature(tables[feature], feat_ids[:, feature, :], bag_lens[:, feature]), jnp.arange(FEATS, dtype=jnp.int32))
    features = jnp.transpose(pooled, (1, 0, 2)).reshape(USERS, FEATS * E)
    hidden = jnp.maximum(jnp.dot(features, w_hidden, preferred_element_type=jnp.float32) + b_hidden, 0.0).astype(jnp.bfloat16)
    queries = (jnp.dot(hidden, w_out, preferred_element_type=jnp.float32) + b_out).astype(jnp.bfloat16)
    item_index = jnp.arange(ITEMS, dtype=jnp.int32)

    def user_block(item_grads, block_number):
        block_queries = lax.dynamic_slice_in_dim(queries, block_number * UBLK, UBLK, 0)
        wanted = lax.dynamic_slice_in_dim(positives, block_number * UBLK, UBLK, 0)
        allowed = jnp.repeat(elig_mask[block_number] > 0, IBLK)
        scores = jnp.dot(block_queries, item_vecs.T, preferred_element_type=jnp.float32)
        block_max = jnp.max(jnp.where(allowed[None, :], scores, masked_value), axis=1)
        totals = jnp.sum(jnp.where(allowed[None, :], jnp.exp(scores - block_max[:, None]), 0.0), axis=1)
        log_norm = block_max + jnp.log(totals)
        target = item_index[None, :] == wanted[:, None]
        picked = jnp.sum(jnp.where(target, scores, 0.0), axis=1)
        probabilities = jnp.where(allowed[None, :], jnp.exp(scores - log_norm[:, None]), 0.0)
        signal = (probabilities - target.astype(jnp.float32)).astype(jnp.bfloat16)
        user_part = jnp.dot(signal, item_vecs, preferred_element_type=jnp.float32)
        item_grads = item_grads + jnp.dot(signal.T, block_queries, preferred_element_type=jnp.float32)
        return item_grads, (log_norm - picked, user_part)

    item_grad, (losses, user_parts) = lax.scan(user_block, jnp.zeros((ITEMS, DQ), jnp.float32), jnp.arange(USERS // UBLK, dtype=jnp.int32))
    return losses.reshape(USERS), user_parts.reshape(USERS, DQ), item_grad
```

```python
import functools

import jax
import jax.numpy as jnp
from jax import lax
from jax.experimental import pallas as pl
from jax.experimental.pallas import tpu as pltpu
from jax.sharding import PartitionSpec as P

IBLK = 128
masked_value = -1e30


def pool_kernel(ids_a, ids_b, tables_ref, out_ref, rows_ref, sums, *, bag, group, tiles):
    table_rows, width = tables_ref.shape[1:]

    @pl.when(pl.program_id(0) == 0)
    def _():
        rows_ref[:table_rows] = tables_ref[0].astype(jnp.float32)
        rows_ref[table_rows : 2 * table_rows] = tables_ref[1].astype(jnp.float32)
        rows_ref[2 * table_rows :] = jnp.zeros((8, width), jnp.float32)

    def pool_tile(ids, feature, tile):
        base = (tile // 16) * (128 * bag) + (tile % 16) * 8
        for user in range(8):
            terms = [
                rows_ref[pl.ds(ids[base + entry * 128 + user], 1), :] for entry in range(bag)
            ]
            while len(terms) > 1:
                terms = [first + second for first, second in zip(terms[::2], terms[1::2])]
            sums[tile, user : user + 1, feature * width : (feature + 1) * width] = terms[0]

    for feature, ids in enumerate((ids_a, ids_b)):

        def step(index, carry, ids=ids, feature=feature):
            for offset in range(tiles):
                pool_tile(ids, feature, index * tiles + offset)
            return carry

        lax.fori_loop(0, group // 8 // tiles, step, 0)
    out_ref[...] = sums[...].reshape(group, 2 * width).astype(jnp.bfloat16)


def pool(tables, ids, users, bag, group=512, tiles=4):
    features, table_rows, width = tables.shape
    steps = users // group
    return pl.pallas_call(
        functools.partial(pool_kernel, bag=bag, group=group, tiles=tiles),
        grid=(steps,),
        in_specs=[
            pl.BlockSpec((group * bag,), lambda i: (i,), memory_space=pltpu.SMEM),
            pl.BlockSpec((group * bag,), lambda i: (i + steps,), memory_space=pltpu.SMEM),
            pl.BlockSpec(tables.shape, lambda i: (0, 0, 0), pipeline_mode=pl.Buffered(1)),
        ],
        out_specs=pl.BlockSpec((group, 2 * width), lambda i: (i, 0)),
        out_shape=jax.ShapeDtypeStruct((users, 2 * width), jnp.bfloat16),
        scratch_shapes=[
            pltpu.VMEM((2 * table_rows + 8, width), jnp.float32),
            pltpu.VMEM((group // 8, 8, 2 * width), jnp.float32),
        ],
        compiler_params=pltpu.CompilerParams(vmem_limit_bytes=40 << 20),
        cost_estimate=pl.CostEstimate(
            flops=users * 2 * bag * width, bytes_accessed=20 << 20, transcendentals=0
        ),
        name="pool",
    )(ids, ids, tables)


def step_kernel(
    arrived_ref, w_hidden_ref, b_hidden_ref, w_out_ref, b_out_ref, items_ref, allowed_ref,
    positives_ref, loss_ref, user_grad_ref, item_grad_ref, scores_ref, *, chunk
):
    sources, users, width = arrived_ref.shape
    items = items_ref.shape[0]
    chunks = items // chunk

    @pl.when(pl.program_id(0) == 0)
    def _():
        item_grad_ref[...] = jnp.zeros_like(item_grad_ref)

    hidden = jnp.dot(
        arrived_ref[0], w_hidden_ref[:width], preferred_element_type=jnp.float32
    )
    for source in range(1, sources):
        hidden += jnp.dot(
            arrived_ref[source],
            w_hidden_ref[source * width : (source + 1) * width],
            preferred_element_type=jnp.float32,
        )
    hidden = jnp.maximum(hidden + b_hidden_ref[...], 0.0).astype(jnp.bfloat16)
    queries = (
        jnp.dot(hidden, w_out_ref[...], preferred_element_type=jnp.float32) + b_out_ref[...]
    ).astype(jnp.bfloat16)

    wanted = positives_ref[...]
    lane = lax.broadcasted_iota(jnp.int32, (users, chunk), 1)

    def fold(value, op):
        pieces = [value[:, k * 128 : (k + 1) * 128] for k in range(chunk // 128)]
        return functools.reduce(op, pieces)

    best = jnp.full((users, 128), masked_value, jnp.float32)
    chosen = jnp.zeros((users, 128), jnp.float32)
    for index in range(chunks):
        span = slice(index * chunk, (index + 1) * chunk)
        scores = lax.dot_general(
            queries, items_ref[span], (((1,), (1,)), ((), ())), preferred_element_type=jnp.float32
        )
        target = lane == wanted - index * chunk
        chosen += fold(jnp.where(target, scores, 0.0), jnp.add)
        scores = jnp.where(allowed_ref[0, :, span] > 0, scores, masked_value)
        best = jnp.maximum(best, fold(scores, jnp.maximum))
        scores_ref[:, span] = scores
    largest = jnp.max(best, axis=1, keepdims=True)
    summed = jnp.zeros((users, 128), jnp.float32)
    for index in range(chunks):
        span = slice(index * chunk, (index + 1) * chunk)
        powers = jnp.exp(scores_ref[:, span] - largest)
        summed += fold(powers, jnp.add)
        scores_ref[:, span] = powers
    total = jnp.sum(summed, axis=1, keepdims=True)
    loss_ref[...] = largest + jnp.log(total) - jnp.sum(chosen, axis=1, keepdims=True)
    scale = 1.0 / total
    user_grad = jnp.zeros(user_grad_ref.shape, jnp.float32)
    for index in range(chunks):
        span = slice(index * chunk, (index + 1) * chunk)
        target = lane == wanted - index * chunk
        signal = (scores_ref[:, span] * scale - jnp.where(target, 1.0, 0.0)).astype(jnp.bfloat16)
        user_grad += jnp.dot(signal, items_ref[span], preferred_element_type=jnp.float32)
        item_grad_ref[span] += lax.dot_general(
            signal, queries, (((0,), (0,)), ((), ())), preferred_element_type=jnp.float32
        )
    user_grad_ref[...] = user_grad


def train_step(arrived, w_hidden, b_hidden, w_out, b_out, items, allowed, positives, tile=256):
    sources, users, width = arrived.shape
    count, embed = items.shape
    hidden = w_hidden.shape[1]
    per_block = users // allowed.shape[0] // tile
    whole = lambda shape: pl.BlockSpec(shape, lambda i: (0,) * len(shape), pipeline_mode=pl.Buffered(1))
    return pl.pallas_call(
        functools.partial(step_kernel, chunk=512),
        grid=(users // tile,),
        in_specs=[
            pl.BlockSpec((sources, tile, width), lambda i: (0, i, 0)),
            whole(w_hidden.shape),
            whole((1, hidden)),
            whole(w_out.shape),
            whole((1, embed)),
            whole(items.shape),
            pl.BlockSpec((1, 1, count), lambda i: (i // per_block, 0, 0)),
            pl.BlockSpec((tile, 1), lambda i: (i, 0)),
        ],
        out_specs=(
            pl.BlockSpec((tile, 1), lambda i: (i, 0)),
            pl.BlockSpec((tile, embed), lambda i: (i, 0)),
            pl.BlockSpec((count, embed), lambda i: (0, 0)),
        ),
        out_shape=(
            jax.ShapeDtypeStruct((users, 1), jnp.float32),
            jax.ShapeDtypeStruct((users, embed), jnp.float32),
            jax.ShapeDtypeStruct((count, embed), jnp.float32),
        ),
        scratch_shapes=[pltpu.VMEM((tile, count), jnp.float32)],
        compiler_params=pltpu.CompilerParams(vmem_limit_bytes=56 << 20),
        cost_estimate=pl.CostEstimate(
            flops=users * (2 * sources * width * hidden + 6 * count * embed),
            bytes_accessed=20 << 20,
            transcendentals=users * count,
        ),
        name="train_step",
    )(
        arrived, w_hidden, b_hidden.reshape(1, -1), w_out, b_out.reshape(1, -1), items,
        allowed[:, None, :], positives[:, None],
    )


def bag_rows(feat_ids, bag_lens, table_rows):
    users, features, bag = feat_ids.shape
    feature = jnp.arange(features, dtype=jnp.int32)[None, :, None]
    counted = jnp.arange(bag, dtype=jnp.int32)[None, None, :] < bag_lens[:, :, None]
    rows = jnp.where(counted, feat_ids + feature * table_rows, features * table_rows)
    rows = rows.transpose(1, 2, 0).reshape(features, bag, users // 128, 128)
    return rows.transpose(0, 2, 1, 3).reshape(-1)


def reduce_items(item_grad):
    rows, embed = item_grad.shape
    item_axis, tbl_axis = lax.axis_size("item"), lax.axis_size("tbl")
    share = rows // item_axis
    pieces = lax.all_to_all(
        item_grad.reshape(item_axis, share, embed), "item", split_axis=0, concat_axis=0
    )
    part = jnp.sum(pieces, axis=0)
    pieces = lax.all_to_all(
        part.reshape(tbl_axis, share // tbl_axis, embed), "tbl", split_axis=0, concat_axis=0
    )
    return jnp.sum(pieces, axis=0)


def local(
    tables, feat_ids, bag_lens, w_hidden, b_hidden, w_out, b_out, item_vecs, elig_mask, positives
):
    table_shards = lax.axis_size("tbl")
    group_users, features, bag = feat_ids.shape
    width = tables.shape[2]
    items = lax.all_gather(item_vecs, "item", axis=0, tiled=True)
    rows = bag_rows(feat_ids, bag_lens, tables.shape[1])
    pooled = pool(tables, rows, group_users, bag)
    pooled = pooled.reshape(table_shards, group_users // table_shards, features * width)
    arrived = lax.all_to_all(pooled, "tbl", split_axis=0, concat_axis=0)
    allowed = jnp.repeat(elig_mask, IBLK, axis=1)
    loss, user_grad, item_part = train_step(
        arrived, w_hidden, b_hidden, w_out, b_out, items, allowed, positives
    )
    return loss[:, 0], user_grad, reduce_items(item_part)


def solution(mesh):
    in_specs = (
        P("tbl", None, None),
        P("item", "tbl", None),
        P("item", "tbl"),
        P(),
        P(),
        P(),
        P(),
        P("item", None),
        P(("item", "tbl"), None),
        P(("item", "tbl")),
    )
    out_specs = (P(("item", "tbl")), P(("item", "tbl"), None), P(("item", "tbl"), None))
    return jax.shard_map(local, mesh=mesh, in_specs=in_specs, out_specs=out_specs, check_vma=False)
```

```python
import functools

import jax
import jax.numpy as jnp
from jax import lax
from jax.experimental import pallas as pl
from jax.experimental.pallas import tpu as pltpu
from jax.sharding import PartitionSpec as P

IBLK = 128
masked_value = -1e30


def pool_kernel(ids_a, ids_b, tables_ref, out_ref, rows_ref, sums, *, bag, group, tiles):
    table_rows, width = tables_ref.shape[1:]

    @pl.when(pl.program_id(0) == 0)
    def _():
        rows_ref[:table_rows] = tables_ref[0].astype(jnp.float32)
        rows_ref[table_rows : 2 * table_rows] = tables_ref[1].astype(jnp.float32)
        rows_ref[2 * table_rows :] = jnp.zeros((8, width), jnp.float32)

    def pool_tile(ids, feature, tile):
        base = (tile // 16) * (128 * bag) + (tile % 16) * 8
        here = ids.at[pl.ds(base, 128 * (bag - 1) + 8)]
        for user in range(8):
            terms = [
                rows_ref[pl.ds(here[entry * 128 + user], 1), :] for entry in range(bag)
            ]
            while len(terms) > 1:
                terms = [first + second for first, second in zip(terms[::2], terms[1::2])]
            sums[tile, user : user + 1, feature * width : (feature + 1) * width] = terms[0]

    for feature, ids in enumerate((ids_a, ids_b)):

        def step(index, carry, ids=ids, feature=feature):
            for offset in range(tiles):
                pool_tile(ids, feature, index * tiles + offset)
            return carry

        lax.fori_loop(0, group // 8 // tiles, step, 0)
    out_ref[0] = sums[...].reshape(group, 2 * width).astype(jnp.bfloat16)


def pool(tables, ids, owners, users, first, count, bag, group=256, tiles=4):
    features, table_rows, width = tables.shape
    blocks, skip, steps = users // group, first // group, count // group
    place = lambda i: (i // steps) * blocks + skip + i % steps
    return pl.pallas_call(
        functools.partial(pool_kernel, bag=bag, group=group, tiles=tiles),
        grid=(owners * steps,),
        in_specs=[
            pl.BlockSpec((group * bag,), lambda i: (place(i),), memory_space=pltpu.SMEM),
            pl.BlockSpec(
                (group * bag,), lambda i: (place(i) + owners * blocks,), memory_space=pltpu.SMEM
            ),
            pl.BlockSpec(tables.shape, lambda i: (0, 0, 0), pipeline_mode=pl.Buffered(1)),
        ],
        out_specs=pl.BlockSpec((1, group, 2 * width), lambda i: (i // steps, i % steps, 0)),
        out_shape=jax.ShapeDtypeStruct((owners, count, 2 * width), jnp.bfloat16),
        scratch_shapes=[
            pltpu.VMEM((2 * table_rows + 8, width), jnp.float32),
            pltpu.VMEM((group // 8, 8, 2 * width), jnp.float32),
        ],
        compiler_params=pltpu.CompilerParams(vmem_limit_bytes=60 << 20),
        cost_estimate=pl.CostEstimate(
            flops=0, bytes_accessed=owners * count * (64 << 10) // 2, transcendentals=0
        ),
        name="pool",
    )(ids, ids, tables)


def step_kernel(
    core_ref, arrived_ref, w_hidden_ref, b_hidden_ref, w_out_ref, b_out_ref, items_ref, allowed_ref,
    positives_ref, *refs, chunk, resumed
):
    if resumed:
        theirs_in, mine_in = refs[2:4]
        refs = refs[4:]
    loss_ref, user_grad_ref, theirs_ref, mine_ref, scores_ref = refs
    sources, users, width = arrived_ref.shape
    items = items_ref.shape[0]
    half = items // chunk // 2
    core = core_ref[0]

    @pl.when(pl.program_id(0) == 0)
    def _():
        if resumed:
            theirs_ref[...] = theirs_in[...]
            mine_ref[...] = mine_in[...]
        else:
            theirs_ref[...] = jnp.zeros_like(theirs_ref)
            mine_ref[...] = jnp.zeros_like(mine_ref)

    hidden = jnp.dot(
        arrived_ref[0], w_hidden_ref[:width], preferred_element_type=jnp.float32
    )
    for source in range(1, sources):
        hidden += jnp.dot(
            arrived_ref[source],
            w_hidden_ref[source * width : (source + 1) * width],
            preferred_element_type=jnp.float32,
        )
    hidden = jnp.maximum(hidden + b_hidden_ref[...], 0.0).astype(jnp.bfloat16)
    queries = (
        jnp.dot(hidden, w_out_ref[...], preferred_element_type=jnp.float32) + b_out_ref[...]
    ).astype(jnp.bfloat16)

    wanted = positives_ref[...]
    lane = lax.broadcasted_iota(jnp.int32, (users, chunk), 1)

    def fold(value, op):
        pieces = [value[:, k * 128 : (k + 1) * 128] for k in range(chunk // 128)]
        return functools.reduce(op, pieces)

    chunks = []
    for keeper in (1 - core, core):
        for index in range(half):
            first = pl.multiple_of((2 * index + keeper) * chunk, chunk)
            chunks.append((len(chunks), first, items_ref[pl.ds(first, chunk)]))

    best = jnp.full((users, 128), masked_value, jnp.float32)
    chosen = jnp.zeros((users, 128), jnp.float32)
    for index, first, vectors in chunks:
        span = slice(index * chunk, (index + 1) * chunk)
        scores = lax.dot_general(
            queries, vectors, (((1,), (1,)), ((), ())), preferred_element_type=jnp.float32
        )
        target = lane == wanted - first
        chosen += fold(jnp.where(target, scores, 0.0), jnp.add)
        open_here = allowed_ref[0, :, pl.ds(first, chunk)] > 0
        scores = jnp.where(open_here, scores, masked_value)
        best = jnp.maximum(best, fold(scores, jnp.maximum))
        scores_ref[:, span] = scores
    largest = jnp.max(best, axis=1, keepdims=True)
    summed = jnp.zeros((users, 128), jnp.float32)
    for index, _, _ in chunks:
        span = slice(index * chunk, (index + 1) * chunk)
        powers = jnp.exp(scores_ref[:, span] - largest)
        summed += fold(powers, jnp.add)
        scores_ref[:, span] = powers
    total = jnp.sum(summed, axis=1, keepdims=True)
    loss_ref[...] = largest + jnp.log(total) - jnp.sum(chosen, axis=1, keepdims=True)
    scale = 1.0 / total
    user_grad = jnp.zeros(user_grad_ref.shape, jnp.float32)
    for index, first, vectors in chunks:
        span = slice(index * chunk, (index + 1) * chunk)
        target = lane == wanted - first
        signal = (scores_ref[:, span] * scale - jnp.where(target, 1.0, 0.0)).astype(jnp.bfloat16)
        user_grad += jnp.dot(signal, vectors, preferred_element_type=jnp.float32)
        grad_ref = theirs_ref if index < half else mine_ref
        grad_ref[index % half] += lax.dot_general(
            signal, queries, (((0,), (0,)), ((), ())), preferred_element_type=jnp.float32
        )
    user_grad_ref[...] = user_grad


def train_step(
    core, arrived, w_hidden, b_hidden, w_out, b_out, items, allowed, positives, first, before=None,
    tile=256, chunk=256
):
    sources, count, width = arrived.shape
    all_users = positives.shape[0]
    all_items, embed = items.shape
    hidden = w_hidden.shape[1]
    per_block = all_users // allowed.shape[0] // tile
    skip = first // tile
    half = all_items // chunk // 2
    whole = lambda shape: pl.BlockSpec(
        shape, lambda i, core: (0,) * len(shape), pipeline_mode=pl.Buffered(1)
    )
    grads = jax.ShapeDtypeStruct((half, chunk, embed), jnp.float32)
    in_specs = [
        pl.BlockSpec((sources, tile, width), lambda i, core: (0, i, 0)),
        whole(w_hidden.shape),
        whole((1, hidden)),
        whole(w_out.shape),
        whole((1, embed)),
        whole(items.shape),
        pl.BlockSpec((1, 1, all_items), lambda i, core: ((i + skip) // per_block, 0, 0)),
        pl.BlockSpec((tile, 1), lambda i, core: (i + skip, 0)),
    ]
    operands = [
        core, arrived, w_hidden, b_hidden.reshape(1, -1), w_out, b_out.reshape(1, -1), items,
        allowed[:, None, :], positives[:, None],
    ]
    aliases = {}
    if before is not None:
        in_specs += [pl.BlockSpec(memory_space=pl.ANY)] * 2 + [whole(grads.shape)] * 2
        aliases = {len(operands): 0, len(operands) + 1: 1}
        operands += list(before)
    return pl.pallas_call(
        functools.partial(step_kernel, chunk=chunk, resumed=before is not None),
        grid_spec=pltpu.PrefetchScalarGridSpec(
            num_scalar_prefetch=1,
            grid=(count // tile,),
            in_specs=in_specs,
            out_specs=(
                pl.BlockSpec((tile, 1), lambda i, core: (i + skip, 0)),
                pl.BlockSpec((tile, embed), lambda i, core: (i + skip, 0)),
                pl.BlockSpec(grads.shape, lambda i, core: (0, 0, 0)),
                pl.BlockSpec(grads.shape, lambda i, core: (0, 0, 0)),
            ),
            scratch_shapes=[pltpu.VMEM((tile, all_items), jnp.float32)],
        ),
        out_shape=(
            jax.ShapeDtypeStruct((all_users, 1), jnp.float32),
            jax.ShapeDtypeStruct((all_users, embed), jnp.float32),
            grads,
            grads,
        ),
        input_output_aliases=aliases,
        compiler_params=pltpu.CompilerParams(vmem_limit_bytes=60 << 20),
        cost_estimate=pl.CostEstimate(
            flops=count * (2 * sources * width * hidden + 6 * all_items * embed),
            bytes_accessed=20 << 20,
            transcendentals=count * all_items,
        ),
        name="train_step",
    )(*operands)


def bag_rows(feat_ids, bag_lens, table_rows):
    users, features, bag = feat_ids.shape
    feature = jnp.arange(features, dtype=jnp.int32)[None, :, None]
    counted = jnp.arange(bag, dtype=jnp.int32)[None, None, :] < bag_lens[:, :, None]
    rows = jnp.where(counted, feat_ids + feature * table_rows, features * table_rows)
    rows = rows.transpose(1, 2, 0).reshape(features, bag, users // 128, 128)
    return rows.transpose(0, 2, 1, 3).reshape(-1)


def reduce_items(theirs, mine):
    cores, members = 2, lax.axis_size("item")
    pairs = [(member, member ^ 1) for member in range(members)]
    part = mine + lax.ppermute(theirs, "item", pairs)
    same_core = [list(range(core, members, cores)) for core in range(cores)]
    pieces = lax.all_to_all(
        part, "item", split_axis=0, concat_axis=0, axis_index_groups=same_core
    )
    part = jnp.sum(pieces, axis=0)
    share, embed = part.shape
    shards = lax.axis_size("tbl")
    pieces = lax.all_to_all(
        part.reshape(shards, share // shards, embed), "tbl", split_axis=0, concat_axis=0
    )
    return jnp.sum(pieces, axis=0)


SPLIT = (768, 256)


def local(
    tables, feat_ids, bag_lens, w_hidden, b_hidden, w_out, b_out, item_vecs, elig_mask, positives
):
    owners = lax.axis_size("tbl")
    bag = feat_ids.shape[2]
    users = positives.shape[0]
    core = (lax.axis_index("item") % 2).reshape(1)
    items = lax.all_gather(item_vecs, "item", axis=0, tiled=True)
    rows = bag_rows(feat_ids, bag_lens, tables.shape[1])
    allowed = jnp.repeat(elig_mask, IBLK, axis=1)
    parts, first = [], 0
    for count in SPLIT:
        pooled = pool(tables, rows, owners, users, first, count, bag)
        parts.append((first, lax.all_to_all(pooled, "tbl", split_axis=0, concat_axis=0)))
        first += count
    outcome = None
    for first, arrived in parts:
        outcome = train_step(
            core, arrived, w_hidden, b_hidden, w_out, b_out, items, allowed, positives, first, outcome
        )
    loss, user_grad, theirs, mine = outcome
    return loss[:, 0], user_grad, reduce_items(theirs, mine)


def solution(mesh):
    in_specs = (
        P("tbl", None, None),
        P("item", "tbl", None),
        P("item", "tbl"),
        P(),
        P(),
        P(),
        P(),
        P("item", None),
        P(("item", "tbl"), None),
        P(("item", "tbl")),
    )
    out_specs = (P(("item", "tbl")), P(("item", "tbl"), None), P(("item", "tbl"), None))
    return jax.shard_map(local, mesh=mesh, in_specs=in_specs, out_specs=out_specs, check_vma=False)
```

```python
import functools

import jax
import jax.numpy as jnp
from jax import lax
from jax.experimental import pallas as pl
from jax.experimental.pallas import tpu as pltpu
from jax.sharding import PartitionSpec as P

IBLK = 128
masked_value = -1e30


def pool_kernel(ids_ref, tables_ref, out_ref, rows_ref, sums, *scratch, bag, place, stride):
    features, table_rows, width = tables_ref.shape
    *bags, arrived = scratch
    group = sums.shape[0]
    step, steps = pl.program_id(0), pl.num_programs(0)

    def fetch(feature, step):
        first = pl.multiple_of(feature * stride + place(step) * group * bag, group * bag)
        return pltpu.make_async_copy(
            ids_ref.at[pl.ds(first, group * bag)], bags[feature], arrived.at[feature]
        )

    @pl.when(step == 0)
    def _():
        for feature in range(features):
            fetch(feature, 0).start()
        for feature in range(features):
            rows_ref[feature * table_rows : (feature + 1) * table_rows] = tables_ref[
                feature
            ].astype(jnp.float32)
        rows_ref[features * table_rows :] = jnp.zeros((8, width), jnp.float32)

    for feature in range(features):
        fetch(feature, step).wait()
        ids = bags[feature]
        for user in range(group):
            terms = [rows_ref[pl.ds(ids[entry * group + user], 1), :] for entry in range(bag)]
            while len(terms) > 1:
                terms = [first + second for first, second in zip(terms[::2], terms[1::2])]
            sums[user : user + 1, feature * width : (feature + 1) * width] = terms[0]

        @pl.when(step + 1 < steps)
        def _(feature=feature):
            fetch(feature, step + 1).start()

    out_ref[0] = sums[...].astype(jnp.bfloat16)


def pool(tables, ids, owners, users, first, count, bag, group=128):
    features, table_rows, width = tables.shape
    blocks, skip, steps = users // group, first // group, count // group
    place = lambda i: (i // steps) * blocks + skip + i % steps
    return pl.pallas_call(
        functools.partial(pool_kernel, bag=bag, place=place, stride=owners * users * bag),
        grid=(owners * steps,),
        in_specs=[
            pl.BlockSpec(memory_space=pl.ANY),
            pl.BlockSpec(tables.shape, lambda i: (0, 0, 0), pipeline_mode=pl.Buffered(1)),
        ],
        out_specs=pl.BlockSpec(
            (1, group, features * width), lambda i: (i // steps, i % steps, 0)
        ),
        out_shape=pltpu.HBM((owners, count, features * width), jnp.bfloat16),
        scratch_shapes=[
            pltpu.VMEM((features * table_rows + 8, width), jnp.float32),
            pltpu.VMEM((group, features * width), jnp.float32),
            *[pltpu.SMEM((group * bag,), jnp.int32)] * features,
            pltpu.SemaphoreType.DMA((features,)),
        ],
        compiler_params=pltpu.CompilerParams(vmem_limit_bytes=60 << 20),
        cost_estimate=pl.CostEstimate(
            flops=0, bytes_accessed=owners * count * (32 << 10), transcendentals=0
        ),
        name="pool",
    )(ids, tables)


def step_kernel(
    core_ref, arrived_ref, w_hidden_ref, b_hidden_ref, w_out_ref, b_out_ref, items_ref, allowed_ref,
    positives_ref, *refs, chunk, resumed
):
    if resumed:
        theirs_in, mine_in = refs[2:4]
        refs = refs[4:]
    loss_ref, user_grad_ref, theirs_ref, mine_ref, scores_ref = refs
    sources, users, width = arrived_ref.shape
    items = items_ref.shape[0]
    half = items // chunk // 2
    core = core_ref[0]

    @pl.when(pl.program_id(0) == 0)
    def _():
        if resumed:
            theirs_ref[...] = theirs_in[...]
            mine_ref[...] = mine_in[...]
        else:
            theirs_ref[...] = jnp.zeros_like(theirs_ref)
            mine_ref[...] = jnp.zeros_like(mine_ref)

    hidden = jnp.dot(
        arrived_ref[0], w_hidden_ref[:width], preferred_element_type=jnp.float32
    )
    for source in range(1, sources):
        hidden += jnp.dot(
            arrived_ref[source],
            w_hidden_ref[source * width : (source + 1) * width],
            preferred_element_type=jnp.float32,
        )
    hidden = jnp.maximum(hidden + b_hidden_ref[...], 0.0).astype(jnp.bfloat16)
    queries = (
        jnp.dot(hidden, w_out_ref[...], preferred_element_type=jnp.float32) + b_out_ref[...]
    ).astype(jnp.bfloat16)

    wanted = positives_ref[...]
    lane = lax.broadcasted_iota(jnp.int32, (users, chunk), 1)

    def fold(value, op):
        pieces = [value[:, k * 128 : (k + 1) * 128] for k in range(chunk // 128)]
        return functools.reduce(op, pieces)

    chunks = []
    for keeper in (1 - core, core):
        for index in range(half):
            first = pl.multiple_of((2 * index + keeper) * chunk, chunk)
            chunks.append((len(chunks), first, items_ref[pl.ds(first, chunk)]))

    best = jnp.full((users, 128), masked_value, jnp.float32)
    chosen = jnp.zeros((users, 128), jnp.float32)
    for index, first, vectors in chunks:
        span = slice(index * chunk, (index + 1) * chunk)
        scores = lax.dot_general(
            queries, vectors, (((1,), (1,)), ((), ())), preferred_element_type=jnp.float32
        )
        target = lane == wanted - first
        chosen += fold(jnp.where(target, scores, 0.0), jnp.add)
        open_here = allowed_ref[0, :, pl.ds(first, chunk)] > 0
        scores = jnp.where(open_here, scores, masked_value)
        best = jnp.maximum(best, fold(scores, jnp.maximum))
        scores_ref[:, span] = scores
    largest = jnp.max(best, axis=1, keepdims=True)
    summed = jnp.zeros((users, 128), jnp.float32)
    for index, _, _ in chunks:
        span = slice(index * chunk, (index + 1) * chunk)
        powers = jnp.exp(scores_ref[:, span] - largest)
        summed += fold(powers, jnp.add)
        scores_ref[:, span] = powers
    total = jnp.sum(summed, axis=1, keepdims=True)
    loss_ref[...] = largest + jnp.log(total) - jnp.sum(chosen, axis=1, keepdims=True)
    scale = 1.0 / total
    user_grad = jnp.zeros(user_grad_ref.shape, jnp.float32)
    for index, first, vectors in chunks:
        span = slice(index * chunk, (index + 1) * chunk)
        target = lane == wanted - first
        signal = (scores_ref[:, span] * scale - jnp.where(target, 1.0, 0.0)).astype(jnp.bfloat16)
        user_grad += jnp.dot(signal, vectors, preferred_element_type=jnp.float32)
        grad_ref = theirs_ref if index < half else mine_ref
        grad_ref[index % half] += lax.dot_general(
            signal, queries, (((0,), (0,)), ((), ())), preferred_element_type=jnp.float32
        )
    user_grad_ref[...] = user_grad


def train_step(
    core, arrived, w_hidden, b_hidden, w_out, b_out, items, allowed, positives, first, before=None,
    tile=256, chunk=256
):
    sources, count, width = arrived.shape
    all_users = positives.shape[0]
    all_items, embed = items.shape
    hidden = w_hidden.shape[1]
    per_block = all_users // allowed.shape[0] // tile
    skip = first // tile
    half = all_items // chunk // 2
    whole = lambda shape: pl.BlockSpec(
        shape, lambda i, core: (0,) * len(shape), pipeline_mode=pl.Buffered(1)
    )
    grads = jax.ShapeDtypeStruct((half, chunk, embed), jnp.float32)
    in_specs = [
        pl.BlockSpec((sources, tile, width), lambda i, core: (0, i, 0)),
        whole(w_hidden.shape),
        whole((1, hidden)),
        whole(w_out.shape),
        whole((1, embed)),
        whole(items.shape),
        pl.BlockSpec((1, 1, all_items), lambda i, core: ((i + skip) // per_block, 0, 0)),
        pl.BlockSpec((tile, 1), lambda i, core: (i + skip, 0)),
    ]
    operands = [
        core, arrived, w_hidden, b_hidden.reshape(1, -1), w_out, b_out.reshape(1, -1), items,
        allowed[:, None, :], positives[:, None],
    ]
    aliases = {}
    if before is not None:
        in_specs += [pl.BlockSpec(memory_space=pl.ANY)] * 2 + [whole(grads.shape)] * 2
        aliases = {len(operands): 0, len(operands) + 1: 1}
        operands += list(before)
    return pl.pallas_call(
        functools.partial(step_kernel, chunk=chunk, resumed=before is not None),
        grid_spec=pltpu.PrefetchScalarGridSpec(
            num_scalar_prefetch=1,
            grid=(count // tile,),
            in_specs=in_specs,
            out_specs=(
                pl.BlockSpec((tile, 1), lambda i, core: (i + skip, 0)),
                pl.BlockSpec((tile, embed), lambda i, core: (i + skip, 0)),
                pl.BlockSpec(grads.shape, lambda i, core: (0, 0, 0)),
                pl.BlockSpec(grads.shape, lambda i, core: (0, 0, 0)),
            ),
            scratch_shapes=[pltpu.VMEM((tile, all_items), jnp.float32)],
        ),
        out_shape=(
            jax.ShapeDtypeStruct((all_users, 1), jnp.float32),
            jax.ShapeDtypeStruct((all_users, embed), jnp.float32),
            grads,
            grads,
        ),
        input_output_aliases=aliases,
        compiler_params=pltpu.CompilerParams(vmem_limit_bytes=60 << 20),
        cost_estimate=pl.CostEstimate(
            flops=count * (2 * sources * width * hidden + 6 * all_items * embed),
            bytes_accessed=20 << 20,
            transcendentals=count * all_items,
        ),
        name="train_step",
    )(*operands)


def bag_rows(feat_ids, bag_lens, table_rows):
    users, features, bag = feat_ids.shape
    feature = jnp.arange(features, dtype=jnp.int32)[None, :, None]
    counted = jnp.arange(bag, dtype=jnp.int32)[None, None, :] < bag_lens[:, :, None]
    rows = jnp.where(counted, feat_ids + feature * table_rows, features * table_rows)
    rows = rows.transpose(1, 2, 0).reshape(features, bag, users // 128, 128)
    return rows.transpose(0, 2, 1, 3).reshape(-1)


def reduce_items(theirs, mine):
    cores, members = 2, lax.axis_size("item")
    pairs = [(member, member ^ 1) for member in range(members)]
    part = (mine + lax.ppermute(theirs, "item", pairs)).astype(jnp.bfloat16)
    same_core = [list(range(core, members, cores)) for core in range(cores)]
    pieces = lax.all_to_all(
        part, "item", split_axis=0, concat_axis=0, axis_index_groups=same_core
    )
    part = jnp.sum(pieces.astype(jnp.float32), axis=0)
    share, embed = part.shape
    shards = lax.axis_size("tbl")
    pieces = lax.all_to_all(
        part.reshape(shards, share // shards, embed), "tbl", split_axis=0, concat_axis=0
    )
    return jnp.sum(pieces, axis=0)


SPLIT = (512, 512)


def local(
    tables, feat_ids, bag_lens, w_hidden, b_hidden, w_out, b_out, item_vecs, elig_mask, positives
):
    owners = lax.axis_size("tbl")
    bag = feat_ids.shape[2]
    users = positives.shape[0]
    core = (lax.axis_index("item") % 2).reshape(1)
    items = lax.all_gather(item_vecs, "item", axis=0, tiled=True)
    rows = bag_rows(feat_ids, bag_lens, tables.shape[1])
    allowed = jnp.repeat(elig_mask, IBLK, axis=1)
    parts, first = [], 0
    for count in SPLIT:
        pooled = pool(tables, rows, owners, users, first, count, bag)
        parts.append((first, lax.all_to_all(pooled, "tbl", split_axis=0, concat_axis=0)))
        first += count
    outcome = None
    for first, arrived in parts:
        outcome = train_step(
            core, arrived, w_hidden, b_hidden, w_out, b_out, items, allowed, positives, first, outcome
        )
    loss, user_grad, theirs, mine = outcome
    return loss[:, 0], user_grad, reduce_items(theirs, mine)


def solution(mesh):
    in_specs = (
        P("tbl", None, None),
        P("item", "tbl", None),
        P("item", "tbl"),
        P(),
        P(),
        P(),
        P(),
        P("item", None),
        P(("item", "tbl"), None),
        P(("item", "tbl")),
    )
    out_specs = (P(("item", "tbl")), P(("item", "tbl"), None), P(("item", "tbl"), None))
    return jax.shard_map(local, mesh=mesh, in_specs=in_specs, out_specs=out_specs, check_vma=False)
```

```python
import functools

import jax
import jax.numpy as jnp
from jax import lax
from jax.experimental import pallas as pl
from jax.experimental.pallas import tpu as pltpu
from jax.sharding import PartitionSpec as P

IBLK = 128
masked_value = -1e30


def pool_kernel(ids_ref, tables_ref, out_ref, rows_ref, sums, *scratch, bag, place, stride):
    features, table_rows, width = tables_ref.shape
    *bags, arrived = scratch
    group = sums.shape[0]
    step, steps = pl.program_id(0), pl.num_programs(0)

    def fetch(feature, step):
        first = pl.multiple_of(feature * stride + place(step) * group * bag, group * bag)
        return pltpu.make_async_copy(
            ids_ref.at[pl.ds(first, group * bag)], bags[feature], arrived.at[feature]
        )

    @pl.when(step == 0)
    def _():
        for feature in range(features):
            fetch(feature, 0).start()
        for feature in range(features):
            rows_ref[feature * table_rows : (feature + 1) * table_rows] = tables_ref[
                feature
            ].astype(jnp.float32)
        rows_ref[features * table_rows :] = jnp.zeros((8, width), jnp.float32)

    for feature in range(features):
        fetch(feature, step).wait()
        ids = bags[feature]
        for user in range(group):
            terms = [rows_ref[pl.ds(ids[entry * group + user], 1), :] for entry in range(bag)]
            while len(terms) > 1:
                terms = [first + second for first, second in zip(terms[::2], terms[1::2])]
            sums[user : user + 1, feature * width : (feature + 1) * width] = terms[0]

        @pl.when(step + 1 < steps)
        def _(feature=feature):
            fetch(feature, step + 1).start()

    out_ref[0] = sums[...].astype(jnp.bfloat16)


def pool(tables, ids, owners, users, first, count, bag, group=128):
    features, table_rows, width = tables.shape
    blocks, skip, steps = users // group, first // group, count // group
    place = lambda i: (i // steps) * blocks + skip + i % steps
    return pl.pallas_call(
        functools.partial(pool_kernel, bag=bag, place=place, stride=owners * users * bag),
        grid=(owners * steps,),
        in_specs=[
            pl.BlockSpec(memory_space=pl.ANY),
            pl.BlockSpec(tables.shape, lambda i: (0, 0, 0), pipeline_mode=pl.Buffered(1)),
        ],
        out_specs=pl.BlockSpec(
            (1, group, features * width), lambda i: (i // steps, i % steps, 0)
        ),
        out_shape=pltpu.HBM((owners, count, features * width), jnp.bfloat16),
        scratch_shapes=[
            pltpu.VMEM((features * table_rows + 8, width), jnp.float32),
            pltpu.VMEM((group, features * width), jnp.float32),
            *[pltpu.SMEM((group * bag,), jnp.int32)] * features,
            pltpu.SemaphoreType.DMA((features,)),
        ],
        compiler_params=pltpu.CompilerParams(vmem_limit_bytes=60 << 20),
        cost_estimate=pl.CostEstimate(
            flops=0, bytes_accessed=owners * count * (32 << 10), transcendentals=0
        ),
        name="pool",
    )(ids, tables)


def step_kernel(
    core_ref, arrived_ref, w_hidden_ref, b_hidden_ref, w_out_ref, b_out_ref, items_ref, allowed_ref,
    positives_ref, *refs, chunk, first_user, block, cuts, resumed
):
    if resumed:
        theirs_in, mine_in = refs[1:3]
        refs = refs[3:]
    loss_ref, user_grad_ref, theirs_ref, mine_ref, scores_ref = refs
    sources, users, width = arrived_ref.shape
    items = items_ref.shape[0]
    half = items // chunk // 2
    core = core_ref[0]
    start = first_user + pl.program_id(0) * users

    if not resumed:

        @pl.when(pl.program_id(0) == 0)
        def _():
            theirs_ref[...] = jnp.zeros_like(theirs_ref)
            mine_ref[...] = jnp.zeros_like(mine_ref)

    hidden = jnp.dot(
        arrived_ref[0], w_hidden_ref[:width], preferred_element_type=jnp.float32
    )
    for source in range(1, sources):
        hidden += jnp.dot(
            arrived_ref[source],
            w_hidden_ref[source * width : (source + 1) * width],
            preferred_element_type=jnp.float32,
        )
    hidden = jnp.maximum(hidden + b_hidden_ref[...], 0.0).astype(jnp.bfloat16)
    queries = (
        jnp.dot(hidden, w_out_ref[...], preferred_element_type=jnp.float32) + b_out_ref[...]
    ).astype(jnp.bfloat16)

    wanted = positives_ref[...]
    lane = lax.broadcasted_iota(jnp.int32, (users, chunk), 1)

    def fold(value, op):
        pieces = [value[:, k * 128 : (k + 1) * 128] for k in range(chunk // 128)]
        return functools.reduce(op, pieces)

    chunks = []
    for keeper in (1 - core, core):
        for index in range(half):
            first = pl.multiple_of((2 * index + keeper) * chunk, chunk)
            chunks.append((len(chunks), first, items_ref[pl.ds(first, chunk)]))

    segments = [(low, high, (start + low) // block) for low, high in zip(cuts[:-1], cuts[1:])]
    best = jnp.full((users, 128), masked_value, jnp.float32)
    chosen = jnp.zeros((users, 128), jnp.float32)
    for index, first, vectors in chunks:
        span = slice(index * chunk, (index + 1) * chunk)
        scores = lax.dot_general(
            queries, vectors, (((1,), (1,)), ((), ())), preferred_element_type=jnp.float32
        )
        target = lane == wanted - first
        chosen += fold(jnp.where(target, scores, 0.0), jnp.add)
        parts = []
        for low, high, row in segments:
            open_here = allowed_ref[row, :, pl.ds(first, chunk)] > 0
            parts.append(jnp.where(open_here, scores[low:high], masked_value))
        scores = parts[0] if len(parts) == 1 else jnp.concatenate(parts, axis=0)
        best = jnp.maximum(best, fold(scores, jnp.maximum))
        scores_ref[:, span] = scores
    largest = jnp.max(best, axis=1, keepdims=True)
    summed = jnp.zeros((users, 128), jnp.float32)
    for index, _, _ in chunks:
        span = slice(index * chunk, (index + 1) * chunk)
        powers = jnp.exp(scores_ref[:, span] - largest)
        summed += fold(powers, jnp.add)
        scores_ref[:, span] = powers
    total = jnp.sum(summed, axis=1, keepdims=True)
    loss_ref[...] = largest + jnp.log(total) - jnp.sum(chosen, axis=1, keepdims=True)
    scale = 1.0 / total
    user_grad = jnp.zeros(user_grad_ref.shape, jnp.float32)
    for index, first, vectors in chunks:
        span = slice(index * chunk, (index + 1) * chunk)
        target = lane == wanted - first
        signal = (scores_ref[:, span] * scale - jnp.where(target, 1.0, 0.0)).astype(jnp.bfloat16)
        user_grad += jnp.dot(signal, vectors, preferred_element_type=jnp.float32)
        grad = lax.dot_general(
            signal, queries, (((0,), (0,)), ((), ())), preferred_element_type=jnp.float32
        )
        place = index % half
        if resumed:
            before, grad_ref = (theirs_in, theirs_ref) if index < half else (mine_in, mine_ref)
            grad_ref[place] = (before[place] + grad).astype(grad_ref.dtype)
        else:
            grad_ref = theirs_ref if index < half else mine_ref
            grad_ref[place] += grad
    user_grad_ref[...] = user_grad


def train_step(
    core, arrived, w_hidden, b_hidden, w_out, b_out, items, allowed, positives, first, tile,
    before=None, chunk=256
):
    sources, count, width = arrived.shape
    all_users = positives.shape[0]
    all_items, embed = items.shape
    hidden = w_hidden.shape[1]
    block = all_users // allowed.shape[0]
    cuts = {0, tile}
    for step in range(count // tile):
        low = first + step * tile
        cuts |= {edge - low for edge in range(block, all_users, block) if low < edge < low + tile}
    half = all_items // chunk // 2
    last = before is not None
    whole = lambda shape: pl.BlockSpec(
        shape, lambda i, core: (0,) * len(shape), pipeline_mode=pl.Buffered(1)
    )
    grads = (half, chunk, embed)
    in_specs = [
        pl.BlockSpec((sources, tile, width), lambda i, core: (0, i, 0)),
        whole(w_hidden.shape),
        whole((1, hidden)),
        whole(w_out.shape),
        whole((1, embed)),
        whole(items.shape),
        whole((allowed.shape[0], 1, all_items)),
        pl.BlockSpec((tile, 1), lambda i, core: (i, 0)),
    ]
    operands = [
        core, arrived, w_hidden, b_hidden.reshape(1, -1), w_out, b_out.reshape(1, -1), items,
        allowed[:, None, :], positives[first : first + count, None],
    ]
    aliases = {}
    if last:
        if count != tile:
            raise ValueError("one step")
        in_specs += [pl.BlockSpec(memory_space=pl.ANY), whole(grads), whole(grads)]
        aliases = {len(operands): 1}
        operands += list(before)
    return pl.pallas_call(
        functools.partial(
            step_kernel, chunk=chunk, first_user=first, block=block, cuts=sorted(cuts), resumed=last
        ),
        grid_spec=pltpu.PrefetchScalarGridSpec(
            num_scalar_prefetch=1,
            grid=(count // tile,),
            in_specs=in_specs,
            out_specs=(
                pl.BlockSpec((tile, 1), lambda i, core: (i, 0)),
                pl.BlockSpec(
                    (pl.Element(tile), pl.Element(embed)), lambda i, core: (pl.multiple_of(first + i * tile, 8), 0)
                ),
                pl.BlockSpec(grads, lambda i, core: (0, 0, 0), pipeline_mode=pl.Buffered(1)),
                pl.BlockSpec(grads, lambda i, core: (0, 0, 0), pipeline_mode=pl.Buffered(1)),
            ),
            scratch_shapes=[pltpu.VMEM((tile, all_items), jnp.float32)],
        ),
        out_shape=(
            jax.ShapeDtypeStruct((count, 1), jnp.float32),
            jax.ShapeDtypeStruct((all_users, embed), jnp.float32),
            jax.ShapeDtypeStruct(grads, jnp.bfloat16 if last else jnp.float32),
            jax.ShapeDtypeStruct(grads, jnp.float32),
        ),
        input_output_aliases=aliases,
        compiler_params=pltpu.CompilerParams(vmem_limit_bytes=60 << 20),
        cost_estimate=pl.CostEstimate(
            flops=count * (2 * sources * width * hidden + 6 * all_items * embed),
            bytes_accessed=20 << 20,
            transcendentals=count * all_items,
        ),
        name="train_step",
    )(*operands)


def bag_rows(feat_ids, bag_lens, table_rows):
    users, features, bag = feat_ids.shape
    feature = jnp.arange(features, dtype=jnp.int32)[None, :, None]
    counted = jnp.arange(bag, dtype=jnp.int32)[None, None, :] < bag_lens[:, :, None]
    rows = jnp.where(counted, feat_ids + feature * table_rows, features * table_rows)
    rows = rows.transpose(1, 2, 0).reshape(features, bag, users // 128, 128)
    return rows.transpose(0, 2, 1, 3).reshape(-1)


def reduce_items(theirs, mine):
    cores, members = 2, lax.axis_size("item")
    pairs = [(member, member ^ 1) for member in range(members)]
    part = (mine + lax.ppermute(theirs, "item", pairs).astype(jnp.float32)).astype(jnp.bfloat16)
    same_core = [list(range(core, members, cores)) for core in range(cores)]
    pieces = lax.all_to_all(
        part, "item", split_axis=0, concat_axis=0, axis_index_groups=same_core
    )
    part = jnp.sum(pieces.astype(jnp.float32), axis=0)
    share, embed = part.shape
    shards = lax.axis_size("tbl")
    pieces = lax.all_to_all(
        part.reshape(shards, share // shards, embed), "tbl", split_axis=0, concat_axis=0
    )
    return jnp.sum(pieces, axis=0)


SPLIT = ((640, 320), (384, 384))


def local(
    tables, feat_ids, bag_lens, w_hidden, b_hidden, w_out, b_out, item_vecs, elig_mask, positives
):
    owners = lax.axis_size("tbl")
    bag = feat_ids.shape[2]
    users = positives.shape[0]
    core = (lax.axis_index("item") % 2).reshape(1)
    items = lax.all_gather(item_vecs, "item", axis=0, tiled=True)
    rows = bag_rows(feat_ids, bag_lens, tables.shape[1])
    allowed = jnp.repeat(elig_mask, IBLK, axis=1)
    parts, first = [], 0
    for count, tile in SPLIT:
        pooled = pool(tables, rows, owners, users, first, count, bag)
        parts.append((first, tile, lax.all_to_all(pooled, "tbl", split_axis=0, concat_axis=0)))
        first += count
    losses, before = [], None
    for first, tile, arrived in parts:
        loss, *before = train_step(
            core, arrived, w_hidden, b_hidden, w_out, b_out, items, allowed, positives, first, tile,
            before,
        )
        losses.append(loss[:, 0])
    user_grad, theirs, mine = before
    return jnp.concatenate(losses), user_grad, reduce_items(theirs, mine)


def solution(mesh):
    in_specs = (
        P("tbl", None, None),
        P("item", "tbl", None),
        P("item", "tbl"),
        P(),
        P(),
        P(),
        P(),
        P("item", None),
        P(("item", "tbl"), None),
        P(("item", "tbl")),
    )
    out_specs = (P(("item", "tbl")), P(("item", "tbl"), None), P(("item", "tbl"), None))
    return jax.shard_map(local, mesh=mesh, in_specs=in_specs, out_specs=out_specs, check_vma=False)
```

```python
import functools

import jax
import jax.numpy as jnp
from jax import lax
from jax.experimental import pallas as pl
from jax.experimental.pallas import tpu as pltpu
from jax.sharding import PartitionSpec as P

IBLK = 128
masked_value = -1e30


def pool_kernel(
    ids_ref, tables_hbm, out_ref, tables_ref, rows_ref, sums, *scratch, bag, place, stride
):
    features, table_rows, width = tables_ref.shape
    *bags, arrived, loaded = scratch
    pieces = loaded.shape[0] // features
    depth = table_rows // pieces
    group = bags[0].shape[0] // bag
    slots = len(bags)
    step, steps = pl.program_id(0), pl.num_programs(0)

    def fetch(slot, step):
        block, feature = slot // features, slot % features
        block = step * (slots // features) + block
        first = pl.multiple_of(feature * stride + place(block) * group * bag, group * bag)
        return pltpu.make_async_copy(
            ids_ref.at[pl.ds(first, group * bag)], bags[slot], arrived.at[slot]
        )

    @pl.when(step == 0)
    def _():
        for slot in range(slots):
            fetch(slot, 0).start()
        loads = []
        for piece in range(features * pieces):
            feature, low = piece // pieces, piece % pieces * depth
            loads.append(
                pltpu.make_async_copy(
                    tables_hbm.at[feature, pl.ds(low, depth)],
                    tables_ref.at[feature, pl.ds(low, depth)],
                    loaded.at[piece],
                )
            )
            loads[-1].start()
        for piece, load in enumerate(loads):
            feature, low = piece // pieces, piece % pieces * depth
            load.wait()
            rows_ref[piece * depth : (piece + 1) * depth] = tables_ref[
                feature, low : low + depth
            ].astype(jnp.float32)
        rows_ref[features * table_rows :] = jnp.zeros((8, width), jnp.float32)

    for slot in range(slots):
        fetch(slot, step).wait()
        ids, feature, low = bags[slot], slot % features, slot // features * group
        for user in range(group):
            terms = [rows_ref[pl.ds(ids[entry * group + user], 1), :] for entry in range(bag)]
            while len(terms) > 1:
                terms = [first + second for first, second in zip(terms[::2], terms[1::2])]
            row = slice(low + user, low + user + 1)
            sums[row, feature * width : (feature + 1) * width] = terms[0]

        @pl.when(step + 1 < steps)
        def _(slot=slot):
            fetch(slot, step + 1).start()

    out_ref[...] = sums[...].astype(jnp.bfloat16)


def pool(tables, ids, owners, users, first, count, bag, group=128, groups=2, pieces=8):
    features, table_rows, width = tables.shape
    blocks, skip, steps = users // group, first // group, count // group
    place = lambda i: (i // steps) * blocks + skip + i % steps
    return pl.pallas_call(
        functools.partial(pool_kernel, bag=bag, place=place, stride=owners * users * bag),
        grid=(owners * steps // groups,),
        in_specs=[
            pl.BlockSpec(memory_space=pl.ANY),
            pl.BlockSpec(memory_space=pl.ANY),
        ],
        out_specs=pl.BlockSpec((groups * group, features * width), lambda i: (i, 0)),
        out_shape=pltpu.HBM((owners * count, features * width), jnp.bfloat16),
        scratch_shapes=[
            pltpu.VMEM(tables.shape, tables.dtype),
            pltpu.VMEM((features * table_rows + 8, width), jnp.float32),
            pltpu.VMEM((groups * group, features * width), jnp.float32),
            *[pltpu.SMEM((group * bag,), jnp.int32)] * (features * groups),
            pltpu.SemaphoreType.DMA((features * groups,)),
            pltpu.SemaphoreType.DMA((features * pieces,)),
        ],
        compiler_params=pltpu.CompilerParams(vmem_limit_bytes=60 << 20),
        cost_estimate=pl.CostEstimate(
            flops=0, bytes_accessed=owners * count * (32 << 10), transcendentals=0
        ),
        name="pool",
    )(ids, tables).reshape(owners, count, features * width)


def step_kernel(
    core_ref, eligible_ref, arrived_ref, w_hidden_hbm, b_hidden_ref, w_out_ref, b_out_ref, items_hbm,
    positives_ref, *refs, chunk, first_user, block, cuts, resumed
):
    if resumed:
        theirs_hbm, mine_hbm = refs[1:3]
        refs = refs[3:]
    (
        loss_ref, user_grad_ref, theirs_ref, mine_ref, scores_ref, w_hidden_ref, items_ref, *before,
        w_loaded, loaded,
    ) = refs
    sources, users, width = arrived_ref.shape
    weights = [
        pltpu.make_async_copy(
            w_hidden_hbm.at[pl.ds(source * width, width)],
            w_hidden_ref.at[pl.ds(source * width, width)],
            w_loaded.at[source],
        )
        for source in range(sources)
    ]
    loads = [pltpu.make_async_copy(items_hbm, items_ref, loaded.at[0])]
    if resumed:
        theirs_in, mine_in = before
        loads.append(pltpu.make_async_copy(theirs_hbm, theirs_in, loaded.at[1]))
        loads.append(pltpu.make_async_copy(mine_hbm, mine_in, loaded.at[2]))

    def on_entry(action):
        if resumed:
            action()
        else:
            pl.when(pl.program_id(0) == 0)(action)

    @on_entry
    def _():
        for copy in weights + loads:
            copy.start()

    items = items_ref.shape[0]
    half = items // chunk // 2
    core = core_ref[0]
    start = first_user + pl.program_id(0) * users

    if not resumed:

        @pl.when(pl.program_id(0) == 0)
        def _():
            theirs_ref[...] = jnp.zeros_like(theirs_ref)
            mine_ref[...] = jnp.zeros_like(mine_ref)

    on_entry(weights[0].wait)
    hidden = jnp.dot(
        arrived_ref[0], w_hidden_ref[:width], preferred_element_type=jnp.float32
    )
    for source in range(1, sources):
        on_entry(weights[source].wait)
        hidden += jnp.dot(
            arrived_ref[source],
            w_hidden_ref[source * width : (source + 1) * width],
            preferred_element_type=jnp.float32,
        )
    hidden = jnp.maximum(hidden + b_hidden_ref[...], 0.0).astype(jnp.bfloat16)
    queries = (
        jnp.dot(hidden, w_out_ref[...], preferred_element_type=jnp.float32) + b_out_ref[...]
    ).astype(jnp.bfloat16)

    on_entry(loads[0].wait)
    wanted = positives_ref[...]
    lane = lax.broadcasted_iota(jnp.int32, (users, chunk), 1)

    def fold(value, op):
        pieces = [value[:, k * 128 : (k + 1) * 128] for k in range(chunk // 128)]
        return functools.reduce(op, pieces)

    chunks = []
    for keeper in (1 - core, core):
        for index in range(half):
            first = pl.multiple_of((2 * index + keeper) * chunk, chunk)
            chunks.append((len(chunks), first))

    segments = [(low, high, (start + low) // block) for low, high in zip(cuts[:-1], cuts[1:])]
    best = jnp.full((users, 128), masked_value, jnp.float32)
    chosen = jnp.zeros((users, 128), jnp.float32)
    for index, first in chunks:
        vectors = items_ref[pl.ds(first, chunk)]
        span = slice(index * chunk, (index + 1) * chunk)
        scores = lax.dot_general(
            queries, vectors, (((1,), (1,)), ((), ())), preferred_element_type=jnp.float32
        )
        target = lane == wanted - first
        for column in range(chunk // 128):
            lanes = slice(column * 128, (column + 1) * 128)
            chosen = jnp.where(target[:, lanes], scores[:, lanes], chosen)
        parts = []
        for low, high, row in segments:
            columns = []
            for column in range(chunk // IBLK):
                open_here = eligible_ref[row, first // IBLK + column] > 0
                bias = jnp.where(open_here, 0.0, masked_value)
                lanes = slice(column * IBLK, (column + 1) * IBLK)
                columns.append(scores[low:high, lanes] + bias)
            parts.append(jnp.concatenate(columns, axis=1))
        scores = parts[0] if len(parts) == 1 else jnp.concatenate(parts, axis=0)
        best = jnp.maximum(best, fold(scores, jnp.maximum))
        scores_ref[:, span] = scores
    largest = jnp.max(best, axis=1, keepdims=True)
    summed = jnp.zeros((users, 128), jnp.float32)
    for index, _ in chunks:
        span = slice(index * chunk, (index + 1) * chunk)
        powers = jnp.exp(scores_ref[:, span] - largest)
        summed += fold(powers, jnp.add)
        scores_ref[:, span] = powers
    total = jnp.sum(summed, axis=1, keepdims=True)
    loss_ref[...] = largest + jnp.log(total) - jnp.sum(chosen, axis=1, keepdims=True)
    scale = 1.0 / total
    user_grad = jnp.zeros(user_grad_ref.shape, jnp.float32)
    for load in loads[1:]:
        load.wait()
    for index, first in chunks:
        vectors = items_ref[pl.ds(first, chunk)]
        span = slice(index * chunk, (index + 1) * chunk)
        target = lane == wanted - first
        signal = (scores_ref[:, span] * scale - jnp.where(target, 1.0, 0.0)).astype(jnp.bfloat16)
        user_grad += jnp.dot(signal, vectors, preferred_element_type=jnp.float32)
        grad = lax.dot_general(
            signal, queries, (((0,), (0,)), ((), ())), preferred_element_type=jnp.float32
        )
        place = index % half
        if resumed:
            before, grad_ref = (theirs_in, theirs_ref) if index < half else (mine_in, mine_ref)
            grad_ref[place] = (before[place] + grad).astype(grad_ref.dtype)
        else:
            grad_ref = theirs_ref if index < half else mine_ref
            grad_ref[place] += grad
    user_grad_ref[...] = user_grad


def train_step(
    core, arrived, w_hidden, b_hidden, w_out, b_out, items, eligible, positives, first, tile,
    before=None, chunk=256
):
    sources, count, width = arrived.shape
    all_users = positives.shape[0]
    all_items, embed = items.shape
    hidden = w_hidden.shape[1]
    block = all_users // eligible.shape[0]
    cuts = {0, tile}
    for step in range(count // tile):
        low = first + step * tile
        cuts |= {edge - low for edge in range(block, all_users, block) if low < edge < low + tile}
    half = all_items // chunk // 2
    last = before is not None
    whole = lambda shape: pl.BlockSpec(
        shape, lambda i, *_: (0,) * len(shape), pipeline_mode=pl.Buffered(1)
    )
    grads = (half, chunk, embed)
    hbm = pl.BlockSpec(memory_space=pl.ANY)
    in_specs = [
        pl.BlockSpec((sources, tile, width), lambda i, *_: (0, i, 0)),
        hbm,
        whole((1, hidden)),
        whole(w_out.shape),
        whole((1, embed)),
        hbm,
        pl.BlockSpec(
            (pl.Element(tile), pl.Element(1)), lambda i, *_: (pl.multiple_of(first + i * tile, 8), 0)
        ),
    ]
    operands = [
        core, eligible, arrived, w_hidden, b_hidden.reshape(1, -1), w_out, b_out.reshape(1, -1), items,
        positives[:, None],
    ]
    aliases = {}
    if last:
        if count != tile:
            raise ValueError("one step")
        in_specs += [hbm] * 3
        aliases = {len(operands): 1}
        operands += list(before)
    return pl.pallas_call(
        functools.partial(
            step_kernel, chunk=chunk, first_user=first, block=block, cuts=sorted(cuts), resumed=last
        ),
        grid_spec=pltpu.PrefetchScalarGridSpec(
            num_scalar_prefetch=2,
            grid=(count // tile,),
            in_specs=in_specs,
            out_specs=(
                pl.BlockSpec((tile, 1), lambda i, *_: (i, 0)),
                pl.BlockSpec(
                    (pl.Element(tile), pl.Element(embed)), lambda i, *_: (pl.multiple_of(first + i * tile, 8), 0)
                ),
                pl.BlockSpec(grads, lambda i, *_: (0, 0, 0), pipeline_mode=pl.Buffered(1)),
                pl.BlockSpec(grads, lambda i, *_: (0, 0, 0), pipeline_mode=pl.Buffered(1)),
            ),
            scratch_shapes=[
                pltpu.VMEM((tile, all_items), jnp.float32),
                pltpu.VMEM(w_hidden.shape, w_hidden.dtype),
                pltpu.VMEM(items.shape, items.dtype),
                *[pltpu.VMEM(grads, jnp.float32)] * (2 if last else 0),
                pltpu.SemaphoreType.DMA((sources,)),
                pltpu.SemaphoreType.DMA((3,)),
            ],
        ),
        out_shape=(
            jax.ShapeDtypeStruct((count, 1), jnp.float32),
            jax.ShapeDtypeStruct((all_users, embed), jnp.float32),
            jax.ShapeDtypeStruct(grads, jnp.bfloat16 if last else jnp.float32),
            jax.ShapeDtypeStruct(grads, jnp.float32),
        ),
        input_output_aliases=aliases,
        compiler_params=pltpu.CompilerParams(vmem_limit_bytes=60 << 20),
        cost_estimate=pl.CostEstimate(
            flops=count * (2 * sources * width * hidden + 6 * all_items * embed),
            bytes_accessed=20 << 20,
            transcendentals=count * all_items,
        ),
        name="train_step",
    )(*operands)


def bag_rows(feat_ids, bag_lens, table_rows):
    users, features, bag = feat_ids.shape
    feature = jnp.arange(features, dtype=jnp.int32)[None, :, None]
    counted = jnp.arange(bag, dtype=jnp.int32)[None, None, :] < bag_lens[:, :, None]
    rows = jnp.where(counted, feat_ids + feature * table_rows, features * table_rows)
    rows = rows.transpose(1, 2, 0).reshape(features, bag, users // 128, 128)
    return rows.transpose(0, 2, 1, 3).reshape(-1)


def reduce_items(theirs, mine):
    cores, members = 2, lax.axis_size("item")
    pairs = [(member, member ^ 1) for member in range(members)]
    part = (mine + lax.ppermute(theirs, "item", pairs).astype(jnp.float32)).astype(jnp.bfloat16)
    same_core = [list(range(core, members, cores)) for core in range(cores)]
    pieces = lax.all_to_all(
        part, "item", split_axis=0, concat_axis=0, axis_index_groups=same_core
    )
    part = jnp.sum(pieces.astype(jnp.float32), axis=0)
    share, embed = part.shape
    shards = lax.axis_size("tbl")
    pieces = lax.all_to_all(
        part.reshape(shards, share // shards, embed), "tbl", split_axis=0, concat_axis=0
    )
    return jnp.sum(pieces, axis=0)


SPLIT = ((640, 320), (384, 384))


def local(
    tables, feat_ids, bag_lens, w_hidden, b_hidden, w_out, b_out, item_vecs, elig_mask, positives
):
    owners = lax.axis_size("tbl")
    bag = feat_ids.shape[2]
    users = positives.shape[0]
    core = (lax.axis_index("item") % 2).reshape(1)
    items = lax.all_gather(item_vecs, "item", axis=0, tiled=True)
    rows = bag_rows(feat_ids, bag_lens, tables.shape[1])
    parts, first = [], 0
    for count, tile in SPLIT:
        pooled = pool(tables, rows, owners, users, first, count, bag)
        parts.append((first, tile, lax.all_to_all(pooled, "tbl", split_axis=0, concat_axis=0)))
        first += count
    losses, before = [], None
    for first, tile, arrived in parts:
        loss, *before = train_step(
            core, arrived, w_hidden, b_hidden, w_out, b_out, items, elig_mask, positives, first, tile,
            before,
        )
        losses.append(loss[:, 0])
    user_grad, theirs, mine = before
    return jnp.concatenate(losses), user_grad, reduce_items(theirs, mine)


def solution(mesh):
    in_specs = (
        P("tbl", None, None),
        P("item", "tbl", None),
        P("item", "tbl"),
        P(),
        P(),
        P(),
        P(),
        P("item", None),
        P(("item", "tbl"), None),
        P(("item", "tbl")),
    )
    out_specs = (P(("item", "tbl")), P(("item", "tbl"), None), P(("item", "tbl"), None))
    return jax.shard_map(local, mesh=mesh, in_specs=in_specs, out_specs=out_specs, check_vma=False)
```
